32 devices in a mesh: frow: 4 (over y, x), fcol: 2 (over core), sub: 4 (over z).
Axes of the slice: x: 2, y: 2, z: 4, core: 2. Of those that a mesh axis runs over, the one named last changes fastest.
Arguments:
- contrib: bfloat16 [4, 8192, 4096], P('sub', 'frow', 'fcol'), may hold values from -6 to 6, as said below
- row_map: int32 [4, 16], replicated, may hold values from -1 to 63, as said below
- front_slot: int32 [64], replicated, may hold values from 0 to 63, as said below
- own_diag: float32 [32768], P('frow'), may hold values from 128 to 256
- pattern: int32 [64, 8], P('frow', ('fcol', 'sub')), may hold values 0 or 1
Outputs:
- window: float32 [32768, 4096], P('frow', ('fcol', 'sub'))
The draws below stay inside these ranges and needn't reach their ends.
Inputs may be any that keep to these rules, and one draw needn't show every extreme that they name: `contrib`: each child's contribution entries. `front_slot`: A permutation of 0 to 63. `row_map`: each child's live rows come first and number 16 - 1 to 16, some child having all 16 live; a child's live entries are distinct; every child has a live row that maps to front block row 0; live row f * 4 + g + m (0 <= m < 1) of a child goes to a front row i with front_slot[i] // 16 = g.
All inputs are finite; a program needn't handle non-finite values. No bound on the sum of `pattern` on one device may be relied on, other than what follows from the above.
Results may differ from the reference program's by a relative error of at most 0.0025.
Values may be sent and summed in bfloat16 or wider, within the bound.
No kernel may reach another device: no remote copies, remote signals or barrier semaphores. Data moves between devices by JAX's collectives and lax.ppermute only.
A program may use at most 192 MiB of HBM per device.

```python
import math
import jax
import jax.numpy as jnp
from jax import lax

BLK = 512
FB = 64
PER = 1
CRD = 4
FRONT = 32768
KIDS = 4
CRB = 16
ROWB = 16
WC = 8


def slot_helper(key):
    return jax.random.permutation(jax.random.fold_in(key, 7), FB).astype(jnp.int32)


def draw_front_slot(key, part):
    return slot_helper(key)


def draw_row_map(key, part):
    slot_order = slot_helper(key)
    owner_count = FB // ROWB
    inverse_slot = jnp.zeros((FB,), jnp.int32).at[slot_order].set(jnp.arange(FB, dtype=jnp.int32))
    first_home = slot_order[0]
    first_owner = first_home // ROWB
    first_place = first_home % ROWB
    key_places = jax.random.fold_in(key, 22)
    key_counts = jax.random.fold_in(key, 23)
    key_full = jax.random.fold_in(key, 24)
    scores = jax.random.randint(key_places, (KIDS, owner_count, ROWB), 0, 1 << 20) * ROWB + jnp.arange(ROWB, dtype=jnp.int32)
    places = jnp.argsort(scores, axis=-1).astype(jnp.int32)
    lead_place = places[:, :, :1]
    is_first_owner = jnp.arange(owner_count)[None, :, None] == first_owner
    is_first_entry = jnp.arange(ROWB)[None, None, :] == 0
    swapped = jnp.where(is_first_entry, first_place, jnp.where(places == first_place, lead_place, places))
    places = jnp.where(is_first_owner, swapped, places)[:, :, :CRD]
    places = places.reshape(KIDS, owner_count, owner_count, PER)
    stored = jnp.arange(owner_count, dtype=jnp.int32)[None, :, None, None] * ROWB + places
    front_rows = inverse_slot[stored]
    front_rows = jnp.transpose(front_rows, (0, 2, 1, 3)).reshape(KIDS, CRB)
    live_count = jax.random.randint(key_counts, (KIDS,), CRB - PER, CRB + 1)
    full_child = jax.random.randint(key_full, (), 0, KIDS)
    live_count = jnp.where(jnp.arange(KIDS) == full_child, CRB, live_count)
    row_number = jnp.arange(CRB)[None, :]
    mapped = jnp.where(row_number < live_count[:, None], front_rows, -1)
    return mapped.astype(jnp.int32)


def draw_contrib(key, part):
    shape = (KIDS, CRB * BLK, WC * BLK)
    values = jax.random.truncated_normal(key, -6.0, 6.0, shape, jnp.float32)
    return values.astype(jnp.bfloat16)


def with_ends(array, rng, smallest, largest):
    place = [jax.random.randint(jax.random.fold_in(rng, axis), (), 0, length) for axis, length in enumerate(array.shape)]
    widest = array.shape.index(max(array.shape))
    beside = place[:widest] + [(place[widest] + 1) % array.shape[widest]] + place[widest + 1:]
    return array.at[tuple(place)].set(smallest).at[tuple(beside)].set(largest)


def shard_levels(stream_key, dims, shards, smallest, top_value):
    def one(position, shards_of):
        steps = jax.random.uniform(jax.random.fold_in(jax.random.fold_in(stream_key, 6), position), (shards_of,), jnp.float32, smallest / len(shards), top_value / len(shards))
        return jnp.repeat(jnp.exp(steps), dims[position] // shards_of).reshape((-1,) + (1,) * (len(dims) - position - 1))

    loudness = one(*shards[0])
    for cut in shards[1:]:
        loudness = loudness * one(*cut)
    return loudness


def setup_inputs(seed: int = 0) -> dict:
    arg_keys = jax.random.split(jax.random.key(seed), 6)
    return {
        "contrib": draw_contrib(jax.random.fold_in(arg_keys[5], 71), 0),
        "row_map": draw_row_map(jax.random.fold_in(arg_keys[5], 71), 0),
        "front_slot": draw_front_slot(jax.random.fold_in(arg_keys[5], 71), 0),
        "own_diag": jnp.clip(jnp.exp(math.log(256.0) - 0.6931472 * jax.random.uniform(arg_keys[3], (FRONT,), jnp.float32) ** shard_levels(arg_keys[3], (FRONT,), ((0, 4),), -0.2, 0.2)), 128.0, 256.0),
        "pattern": with_ends((jax.random.randint(arg_keys[4], (FB, WC), 0, 4) < 3).astype(jnp.int32), jax.random.fold_in(arg_keys[4], 1), 0, 1),
    }


def assemble(contrib, row_map, front_slot, own_diag, index_col):
    start = (index_col * BLK).astype(jnp.int32)
    contribution = lax.dynamic_slice_in_dim(contrib, start, BLK, axis=2).astype(jnp.float32)
    contribution = contribution.reshape(KIDS * CRB, BLK, BLK)
    flat_map = row_map.reshape(-1)
    is_live = flat_map >= 0
    target_rows = jnp.where(is_live, front_slot[jnp.maximum(flat_map, 0)], FB).astype(jnp.int32)
    column = jnp.zeros((FB + 1, BLK, BLK), contribution.dtype).at[target_rows].add(contribution)[:FB]
    home_slot = front_slot[index_col].astype(jnp.int32)
    values = lax.dynamic_index_in_dim(own_diag.reshape(FB, BLK), home_slot, 0, keepdims=False)
    current = lax.dynamic_index_in_dim(column, home_slot, 0, keepdims=False)
    return lax.dynamic_update_index_in_dim(column, current + jnp.diag(values).astype(column.dtype), home_slot, 0)

def reference(contrib, row_map, front_slot, own_diag, pattern):
    first_column = assemble(contrib, row_map, front_slot, own_diag, jnp.int32(0))
    diagonal = first_column[front_slot[0]]
    symmetric = 0.5 * (diagonal + diagonal.T)
    cholesky_factor = jnp.linalg.cholesky(symmetric)
    identity = jnp.eye(BLK, dtype=cholesky_factor.dtype)
    inverse = lax.linalg.triangular_solve(cholesky_factor, identity, left_side=True, lower=True)
    panel = jnp.dot(first_column.reshape(FRONT, BLK).astype(jnp.float32), inverse.T.astype(jnp.float32), precision=lax.Precision.HIGHEST, preferred_element_type=jnp.float32)
    rounded = lax.optimization_barrier(panel.astype(jnp.bfloat16)).astype(jnp.float32)
    window = jnp.zeros((FRONT, WC * BLK), panel.dtype)
    window = lax.dynamic_update_slice(window, panel, (jnp.int32(0), jnp.int32(0)))

    def one_column(index_col, window):
        index_col = jnp.asarray(index_col).astype(jnp.int32)
        column = assemble(contrib, row_map, front_slot, own_diag, index_col).reshape(FRONT, BLK)
        start = (front_slot[index_col] * BLK).astype(jnp.int32)
        column_piece = lax.dynamic_slice_in_dim(rounded, start, BLK, 0)
        update = jnp.dot(rounded.astype(jnp.float32), column_piece.T.astype(jnp.float32), precision=lax.Precision.HIGHEST, preferred_element_type=jnp.float32)
        pattern_gate = jnp.repeat(pattern[:, index_col], BLK).astype(column.dtype)
        result = column - pattern_gate[:, None] * update
        return lax.dynamic_update_slice(window, result.astype(window.dtype), (jnp.int32(0), (index_col * BLK).astype(jnp.int32)))
    return lax.fori_loop(1, WC, one_column, window)
```

```python
import functools

import jax
import jax.numpy as jnp
from jax import lax
from jax.experimental import pallas as pl
from jax.experimental.pallas import tpu as pltpu
from jax.sharding import PartitionSpec as P

BLK = 512
FB = 64
NB = 128
AXES = ("frow", "fcol", "sub")

HIGH = lax.Precision.HIGHEST
NT = (((1,), (1,)), ((), ()))
NN = (((1,), (0,)), ((), ()))


def dot(a, b, dims, precision=None):
    return lax.dot_general(a, b, dims, precision=precision, preferred_element_type=jnp.float32)


def factor_kernel(meta, x_ref, hi_ref, lo_ref, full_ref, s_ref, l_ref, x_inv, a_ref, w_ref):
    owner = meta[0]
    parts = x_ref.shape[0]
    rows = BLK // parts
    diag = jnp.zeros((1, BLK), jnp.float32)
    for d in range(parts):
        at = pl.multiple_of((owner ^ d) * rows, rows)
        s_ref[pl.ds(at, rows), :] = x_ref[d, :rows, :]
        diag = diag + x_ref[d, rows : rows + 1, :]
    whole = s_ref[...]
    i = lax.broadcasted_iota(jnp.int32, (BLK, BLK), 0)
    k = lax.broadcasted_iota(jnp.int32, (BLK, BLK), 1)
    s_ref[...] = 0.5 * (whole + whole.T) + jnp.where(i == k, diag, 0.0)
    x_inv[...] = jnp.zeros_like(x_inv)
    lane = lax.broadcasted_iota(jnp.int32, (NB, NB), 1)
    line = lax.broadcasted_iota(jnp.int32, (NB, NB), 0)
    for b in range(BLK // NB):
        lo, up = b * NB, (b + 1) * NB
        a_ref[...] = s_ref[lo:up, lo:up]
        w_ref[...] = jnp.where(lane == line, 1.0, 0.0)

        def step(j, carry):
            a = a_ref[...]
            row = a_ref[pl.ds(j, 1), :]
            pivot = jnp.sum(jnp.where(lane[:1] == j, row, 0.0), axis=1, keepdims=True)
            scale = lax.rsqrt(pivot)
            scale = scale * (1.5 - 0.5 * pivot * scale * scale)
            column = jnp.sum(jnp.where(lane == j, a, 0.0), axis=1, keepdims=True)
            below = jnp.where(line[:, :1] > j, column * scale, 0.0)
            a_ref[...] = a - below * (row * scale)
            w_row = w_ref[pl.ds(j, 1), :] * scale
            w_ref[...] = w_ref[...] - below * w_row
            w_ref[pl.ds(j, 1), :] = w_row
            return carry

        lax.fori_loop(0, NB, step, 0)
        part = w_ref[...]
        x_inv[lo:up, lo:up] = part
        if b:
            left = dot(l_ref[lo:up, :lo], x_inv[:lo, :lo], NN, HIGH)
            x_inv[lo:up, :lo] = -dot(part, left, NN, HIGH)
        if up < BLK:
            rest = dot(s_ref[up:, lo:up], part, NT, HIGH)
            l_ref[up:, lo:up] = rest
            s_ref[up:, up:] = s_ref[up:, up:] - dot(rest, rest, NT, HIGH)
    turned = x_inv[...].T
    high = turned.astype(jnp.bfloat16)
    hi_ref[...] = high
    lo_ref[...] = (turned - high.astype(jnp.float32)).astype(jnp.bfloat16)
    full_ref[...] = turned


def factor(meta, x):
    whole = pl.BlockSpec(memory_space=pltpu.VMEM)
    shape = jax.ShapeDtypeStruct((BLK, BLK), jnp.bfloat16)
    return pl.pallas_call(
        factor_kernel,
        grid_spec=pltpu.PrefetchScalarGridSpec(
            num_scalar_prefetch=1,
            grid=(),
            in_specs=[whole],
            out_specs=[whole, whole, whole],
            scratch_shapes=[
                pltpu.VMEM((BLK, BLK), jnp.float32),
                pltpu.VMEM((BLK, BLK), jnp.float32),
                pltpu.VMEM((BLK, BLK), jnp.float32),
                pltpu.VMEM((NB, NB), jnp.float32),
                pltpu.VMEM((NB, NB), jnp.float32),
            ],
        ),
        out_shape=[shape, shape, jax.ShapeDtypeStruct((BLK, BLK), jnp.float32)],
        cost_estimate=pl.CostEstimate(flops=int(6e10), bytes_accessed=4 << 20, transcendentals=0),
        name="factor",
    )(meta, x)


def slot_of(row_map, front_slot, owner, owners, owner_blocks, child, holder):
    front = row_map[(child * owners + holder) * owners + owner]
    stored = front_slot[jnp.maximum(front, 0)]
    here = (front >= 0) & (stored // owner_blocks == owner)
    return jnp.where(here, stored - owner * owner_blocks, -1)


def panel_kernel(owners, children, row_map, front_slot, meta, *refs):
    arrays = 2 * children
    piles = refs[:arrays]
    hi_ref, lo_ref, full_ref, own_ref = refs[arrays : arrays + 4]
    out_b, out_f = refs[arrays + 4 : arrays + 6]
    raw, acc, slots, sems = refs[arrays + 6 :]
    half = owners // 2
    p = pl.program_id(0)
    owner, column, child = meta[0], meta[1], meta[2]
    blocks = pl.num_programs(0)

    @pl.when(p == 0)
    def _():
        copies = []
        for n, pile in enumerate(piles):
            of_child = child ^ (n % children)
            carrier = (column & 1) ^ (n // children)
            copy = pltpu.make_async_copy(pile, raw.at[pl.ds(n * half, half)], sems.at[n])
            copy.start()
            copies.append(copy)
            for q in range(half):
                holder = owner ^ (carrier * half + q)
                slots[n * half + q] = slot_of(
                    row_map, front_slot, owner, owners, blocks, of_child, holder
                )
        for copy in copies:
            copy.wait()

    acc[...] = jnp.zeros_like(acc)

    @pl.loop(0, arrays * half)
    def _(n):
        @pl.when(slots[n] == p)
        def _():
            block = raw[n]
            acc[...] += dot(block, hi_ref[...], NN) + dot(block, lo_ref[...], NN)

    @pl.when(front_slot[0] == owner * blocks + p)
    def _():
        acc[...] += own_ref[...] * full_ref[...]

    out_b[...] = acc[...].astype(jnp.bfloat16)

    @pl.when(meta[3] == 1)
    def _():
        out_f[...] = acc[...]


def panel_of(row_map, front_slot, meta, piles, hi, lo, full, own, owners, children, blocks):
    anywhere = pl.BlockSpec(memory_space=pl.ANY)
    whole = pl.BlockSpec(memory_space=pltpu.VMEM)
    count = children * owners
    return pl.pallas_call(
        functools.partial(panel_kernel, owners, children),
        grid_spec=pltpu.PrefetchScalarGridSpec(
            num_scalar_prefetch=3,
            grid=(blocks,),
            in_specs=[anywhere] * len(piles) + [whole] * 4,
            out_specs=[
                pl.BlockSpec((BLK, BLK), lambda p, *_: (p, 0)),
                pl.BlockSpec((BLK, BLK), lambda p, rm, fs, m: (p * m[3], 0)),
            ],
            scratch_shapes=[
                pltpu.VMEM((count, BLK, BLK), jnp.bfloat16),
                pltpu.VMEM((BLK, BLK), jnp.float32),
                pltpu.SMEM((count,), jnp.int32),
                pltpu.SemaphoreType.DMA((len(piles),)),
            ],
        ),
        out_shape=[
            jax.ShapeDtypeStruct((blocks * BLK, BLK), jnp.bfloat16),
            jax.ShapeDtypeStruct((blocks * BLK, BLK), jnp.float32),
        ],
        cost_estimate=pl.CostEstimate(flops=int(2e10), bytes_accessed=24 << 20, transcendentals=0),
        name="panel",
    )(row_map, front_slot, meta, *piles, hi, lo, full, own)


def window_kernel(owners, children, row_map, front_slot, meta, gate, *refs):
    count = owners * children
    contrib = refs[0]
    blocks_in = refs[1:count]
    panel_all = refs[count]
    pieces = refs[count + 1 : count + owners]
    panel_b, panel_f, own_ref, out = refs[count + owners : count + owners + 4]
    raw, piece, slots, sems, piece_sem = refs[count + owners + 4 :]
    p = pl.program_id(0)
    blocks = pl.num_programs(0)
    owner, child, first = meta[0], meta[2], meta[3]
    home = front_slot[meta[4]]
    home_owner = home // blocks

    @pl.when((p == 0) & (first == 0))
    def _():
        copies = []
        for n in range(count):
            if n == 0:
                source = contrib.at[0, pl.ds(owner * BLK, BLK), pl.ds(child * BLK, BLK)]
            else:
                source = blocks_in[n - 1]
            copy = pltpu.make_async_copy(source, raw.at[n], sems.at[n])
            copy.start()
            copies.append(copy)
            slots[n] = slot_of(
                row_map,
                front_slot,
                owner,
                owners,
                blocks,
                child ^ (n // owners),
                owner ^ (n % owners),
            )
        for d in range(owners):

            @pl.when(home_owner == owner ^ d)
            def _():
                if d == 0:
                    at = pl.multiple_of((home - owner * blocks) * BLK, BLK)
                    source = panel_all.at[pl.ds(at, BLK)]
                else:
                    source = pieces[d - 1]
                copy = pltpu.make_async_copy(source, piece, piece_sem)
                copy.start()
                copy.wait()

        for copy in copies:
            copy.wait()

    @pl.when(first == 1)
    def _():
        out[...] = panel_f[...]

    @pl.when(first == 0)
    def _():
        kept = gate[p].astype(jnp.float32)
        out[...] = -kept * dot(panel_b[...], piece[...], NT)

        @pl.loop(0, count)
        def _(n):
            @pl.when(slots[n] == p)
            def _():
                out[...] += raw[n].astype(jnp.float32)

        @pl.when(home == owner * blocks + p)
        def _():
            i = lax.broadcasted_iota(jnp.int32, (BLK, BLK), 0)
            k = lax.broadcasted_iota(jnp.int32, (BLK, BLK), 1)
            out[...] += jnp.where(i == k, own_ref[0], 0.0)


def window_of(row_map, front_slot, meta, gate, contrib, received, panel, panel_f, pieces, own,
              owners, children, blocks):
    anywhere = pl.BlockSpec(memory_space=pl.ANY)
    count = owners * children
    return pl.pallas_call(
        functools.partial(window_kernel, owners, children),
        grid_spec=pltpu.PrefetchScalarGridSpec(
            num_scalar_prefetch=4,
            grid=(blocks,),
            in_specs=[anywhere] * (count + owners)
            + [
                pl.BlockSpec((BLK, BLK), lambda p, rm, fs, m, g: (p * (1 - m[3]), 0)),
                pl.BlockSpec((BLK, BLK), lambda p, rm, fs, m, g: (p * m[3], 0)),
                pl.BlockSpec((1, 1, BLK), lambda p, *_: (p, 0, 0)),
            ],
            out_specs=pl.BlockSpec((BLK, BLK), lambda p, *_: (p, 0)),
            scratch_shapes=[
                pltpu.VMEM((count, BLK, BLK), jnp.bfloat16),
                pltpu.VMEM((BLK, BLK), jnp.bfloat16),
                pltpu.SMEM((count,), jnp.int32),
                pltpu.SemaphoreType.DMA((count,)),
                pltpu.SemaphoreType.DMA,
            ],
        ),
        out_shape=jax.ShapeDtypeStruct((blocks * BLK, BLK), jnp.float32),
        cost_estimate=pl.CostEstimate(flops=int(5e9), bytes_accessed=32 << 20, transcendentals=0),
        name="window",
    )(row_map, front_slot, meta, gate, contrib, *received, panel, *pieces, panel, panel_f, own)


def on_device(contrib, row_map, front_slot, own_diag, pattern):
    owners, columns, children = (lax.axis_size(a) for a in AXES)
    f, j, s = (lax.axis_index(a) for a in AXES)
    blocks = FB // owners
    half = owners // 2
    matrix = contrib[0]
    front_slot = front_slot.astype(jnp.int32)
    row_map = row_map.reshape(-1).astype(jnp.int32)
    column = j * children + s
    first = (column == 0).astype(jnp.int32)
    meta = jnp.stack([f, j, s, first, column]).astype(jnp.int32)

    def move(x, target):
        pairs = []
        for df in range(owners):
            for dj in range(columns):
                for ds in range(children):
                    to = target(df, dj, ds)
                    if to is not None:
                        source = (df * columns + dj) * children + ds
                        pairs.append((source, (to[0] * columns + to[1]) * children + to[2]))
        return lax.ppermute(x, AXES, pairs)

    def block(row, col):
        return lax.dynamic_slice(matrix, (row * BLK, col * BLK), (BLK, BLK))

    home = front_slot[0]
    root = home // blocks
    quarter = BLK // owners
    is_root = (row_map[(s * owners + f) * owners + root] == 0) & (j == 0)
    mine = jnp.where(is_root, block(root, 0), jnp.zeros((), matrix.dtype))
    part = lax.dynamic_slice(mine, (f * quarter, 0), (quarter, BLK))
    for d in range(1, owners):
        sent = lax.dynamic_slice(mine, ((f ^ d) * quarter, 0), (quarter, BLK))
        part = part + move(sent, lambda a, b, c: (a ^ d, b, c) if b == 0 else None)
    total = part.astype(jnp.float32)
    for d in range(1, children):
        total = total + move(part, lambda a, b, c: (a, b, c ^ d) if b == 0 else None).astype(
            jnp.float32
        )
    position = jnp.clip(home - f * blocks, 0, blocks - 1)
    values = lax.dynamic_index_in_dim(own_diag.reshape(blocks, BLK), position, 0)
    values = jnp.where(root == f, values, 0.0)
    total = jnp.concatenate([total, values, jnp.zeros((7, BLK), jnp.float32)], 0)
    quarters = [total]
    for d in range(1, owners):
        quarters.append(move(total, lambda a, b, c: (a ^ d, b, c) if b == 0 else None))
    diagonal = jnp.stack(quarters)
    step = 1
    while step < columns:
        got = move(diagonal, lambda a, b, c: (a, b + step, c) if b < step else None)
        diagonal = jnp.where((j >= step) & (j < 2 * step), got, diagonal)
        step *= 2

    home_blocks = [block(f, 0)]
    for d in range(1, owners):
        home_blocks.append(
            move(
                block(f ^ d, 0),
                lambda a, b, c: (a ^ d, d // half, c) if b == 0 else None,
            )
        )
    pile = jnp.stack(
        [jnp.where(j == 0, home_blocks[q], home_blocks[half + q]) for q in range(half)]
    )
    piles = {0: pile}
    bit = children // 2
    while bit:
        for d in list(piles):
            piles[d ^ bit] = move(
                piles[d], lambda a, b, c: (a, b, c ^ bit) if b < 2 else None
            )
        bit //= 2
    own_piles = [piles[d] for d in range(children)]
    other_piles = [
        move(x, lambda a, b, c: (a, b ^ 1, c) if b < 2 else None) for x in own_piles
    ]
    piles = own_piles + other_piles
    step = 2
    while step < columns:
        here = (j >= step) & (j < 2 * step)
        piles = [
            jnp.where(here, move(x, lambda a, b, c: (a, b + step, c) if b < step else None), x)
            for x in piles
        ]
        step *= 2

    received = {}
    for ds in reversed(range(children)):
        for df in range(owners):
            if ds == 0 and df == 0:
                continue
            received[ds * owners + df] = move(
                block(f ^ df, s ^ ds),
                lambda a, b, c: None if b == 0 and c ^ ds == 0 else (a ^ df, b, c ^ ds),
            )
    received = [received[n] for n in range(1, owners * children)]

    hi, lo, full = factor(meta, diagonal)
    own_root = values.reshape(BLK, 1)
    panel, panel_f = panel_of(
        row_map, front_slot, meta, piles, hi, lo, full, own_root, owners, children, blocks
    )
    home = front_slot[column]
    position = jnp.clip(home - f * blocks, 0, blocks - 1)
    piece = lax.dynamic_slice(panel, (position * BLK, 0), (BLK, BLK))
    pieces = [
        move(piece, lambda a, b, c: None if b == 0 and c == 0 else (a ^ d, b, c))
        for d in range(1, owners)
    ]
    return window_of(
        row_map,
        front_slot,
        meta,
        pattern[:, 0].astype(jnp.int32),
        contrib,
        received,
        panel,
        panel_f,
        pieces,
        own_diag.reshape(blocks, 1, BLK),
        owners,
        children,
        blocks,
    )


def solution(mesh):
    return jax.shard_map(
        on_device,
        mesh=mesh,
        in_specs=(P("sub", "frow", "fcol"), P(), P(), P("frow"), P("frow", ("fcol", "sub"))),
        out_specs=P("frow", ("fcol", "sub")),
        check_vma=False,
    )
```
